32 devices in a mesh: src: 16 (over z, y, core), tgt: 2 (over x).
Axes of the slice: x: 2, y: 2, z: 4, core: 2. Of those that a mesh axis runs over, the one named last changes fastest.
Arguments:
- src_emb: bfloat16 [8192, 1024], P('src', 'tgt'), may hold values from -16 to 16
- tgt_emb: bfloat16 [8192, 1024], P('tgt', 'src'), may hold values from -16 to 16
- src_ids: int32 [8192], P('src'), may hold values from 0 to 4095
- tgt_ids: int32 [8192], P('tgt'), may hold values from 0 to 4095
Outputs:
- margin: float32 [8192, 8192], P('src', 'tgt')
The draws below stay inside these ranges and needn't reach their ends.
All inputs are finite; a program needn't handle non-finite values.
Results may differ from the reference program's by a relative error of at most 0.004.
Values may be sent and summed in bfloat16 or wider, within the bound.
A program may use at most 64 MiB of HBM per device.

```python
import jax
import jax.numpy as jnp
from jax import lax

D = 1024
NEIGH = 4
NS = 8192
NT = 8192


def sentence_tables(key):
    group_rows = jax.random.normal(jax.random.fold_in(key, 11), (NT // 4, D), jnp.float32)
    ident_rows = jax.random.normal(jax.random.fold_in(key, 12), (NT // 2, D), jnp.float32)
    shared_part = jax.random.uniform(jax.random.fold_in(key, 13), (NT // 4,), jnp.float32, 0.1, 0.5)
    own_part = jax.random.uniform(jax.random.fold_in(key, 14), (NT // 2,), jnp.float32, 0.2, 0.45)
    return (group_rows, ident_rows, shared_part, own_part)


def draw_src_ids(key, part):
    return jax.random.randint(jax.random.fold_in(key, 21), (NS,), 0, NT // 2, dtype=jnp.int32)


def draw_tgt_ids(key, part):
    return jax.random.randint(jax.random.fold_in(key, 22), (NT,), 0, NT // 2, dtype=jnp.int32)


def mixed_rows(key, sentence_ids, salt):
    group_rows, ident_rows, shared_part, own_part = sentence_tables(key)
    count = sentence_ids.shape[0]
    group_ids = sentence_ids // 2
    shared_weight = jnp.take(shared_part, group_ids)
    own_weight = jnp.take(own_part, sentence_ids)
    rest_weight = 1.0 - shared_weight - own_weight
    noise_key = jax.random.fold_in(key, salt)
    noise = jax.random.normal(noise_key, (count, D), jnp.float32)
    rows = jnp.sqrt(shared_weight)[:, None] * jnp.take(group_rows, group_ids, axis=0)
    rows = rows + jnp.sqrt(own_weight)[:, None] * jnp.take(ident_rows, sentence_ids, axis=0)
    rows = rows + jnp.sqrt(rest_weight)[:, None] * noise
    return jnp.clip(rows, -16.0, 16.0).astype(jnp.bfloat16)


def draw_src_emb(key, part):
    return mixed_rows(key, draw_src_ids(key, part), 31)


def draw_tgt_emb(key, part):
    return mixed_rows(key, draw_tgt_ids(key, part), 32)


def setup_inputs(seed: int = 0) -> dict:
    keys = jax.random.split(jax.random.key(seed), 5)
    src_emb = draw_src_emb(jax.random.fold_in(keys[4], 71), 0)
    tgt_emb = draw_tgt_emb(jax.random.fold_in(keys[4], 71), 0)
    src_ids = draw_src_ids(jax.random.fold_in(keys[4], 71), 0)
    tgt_ids = draw_tgt_ids(jax.random.fold_in(keys[4], 71), 0)
    return dict(src_emb=src_emb, tgt_emb=tgt_emb, src_ids=src_ids, tgt_ids=tgt_ids)


epsilon = 1e-06
excluded_score = -2.0

def unit_rows(embedded):
    values = embedded.astype(jnp.float32)
    scale = jnp.sqrt(lax.optimization_barrier(jnp.sum(values * values, axis=1, keepdims=True)) + epsilon)
    return (values / scale).astype(jnp.bfloat16)

def best_four(values):
    return lax.top_k(values, NEIGH)[0]

def reference(src_emb, tgt_emb, src_ids, tgt_ids):
    src_unit = unit_rows(src_emb)
    tgt_unit = unit_rows(tgt_emb)
    block_rows = min(512, NS)
    blocks = NS // block_rows
    src_blocks = src_unit.reshape(blocks, block_rows, D)
    id_blocks = src_ids.reshape(blocks, block_rows)

    def cosines(rows, row_ids):
        scores = lax.dot_general(rows, tgt_unit, (((1,), (1,)), ((), ())), preferred_element_type=jnp.float32)
        same = row_ids[:, None] == tgt_ids[None, :]
        return (jnp.where(same, jnp.float32(excluded_score), scores), same)

    def first_pass(column_best, pieces):
        rows, row_ids = pieces
        scores, same = cosines(rows, row_ids)
        row_best = best_four(scores)
        merged = best_four(jnp.concatenate([column_best, best_four(scores.T)], axis=1))
        return (merged, row_best)
    start = jnp.full((NT, NEIGH), excluded_score, jnp.float32)
    column_best, row_best = lax.scan(first_pass, start, (src_blocks, id_blocks))
    knn_src = lax.optimization_barrier(jnp.mean(row_best, axis=-1))
    knn_tgt = lax.optimization_barrier(jnp.mean(column_best, axis=-1))

    def second_pass(pieces):
        rows, row_ids, row_knn = pieces
        scores, same = cosines(rows, row_ids)
        ratio = scores / (0.5 * (row_knn[:, None] + knn_tgt[None, :]))
        return jnp.where(same, jnp.float32(0.0), ratio)
    margin = lax.map(second_pass, (src_blocks, id_blocks, knn_src))
    return margin.reshape(NS, NT)
```

```python
import functools

import jax
import jax.numpy as jnp
from jax import lax
from jax.experimental import pallas as pl
from jax.experimental.pallas import tpu as pltpu
from jax.sharding import PartitionSpec as P

epsilon = 1e-06
excluded_score = -2.0
MESH = pl.DeviceIdType.MESH
CHUNK = 512


def insert(best, value):
    out = []
    for level in best[:-1]:
        out.append(jnp.maximum(level, value))
        value = jnp.minimum(level, value)
    out.append(jnp.maximum(best[-1], value))
    return tuple(out)


def merge(first, second):
    c = [jnp.maximum(first[k], second[3 - k]) for k in range(4)]
    a, b = jnp.maximum(c[0], c[2]), jnp.maximum(c[1], c[3])
    d, e = jnp.minimum(c[0], c[2]), jnp.minimum(c[1], c[3])
    return (jnp.maximum(a, b), jnp.minimum(a, b), jnp.maximum(d, e), jnp.minimum(d, e))


def fold_sublanes(best):
    for shift in (4, 2, 1):
        best = merge(best, tuple(pltpu.roll(level, shift, 0) for level in best))
    return best


def stacked(best):
    row = lax.broadcasted_iota(jnp.int32, best[0].shape, 0)
    low = jnp.full(best[0].shape, -jnp.inf, jnp.float32)
    for k in range(3, -1, -1):
        low = jnp.where(row == k, best[k], low)
    return low


def lowest(shape):
    return tuple(jnp.full(shape, -jnp.inf, jnp.float32) for _ in range(4))


def kernel(dims, x_ref, a_ref, sid_ref, tid_ref, s_out, kt_out, ks_out, g, a_whole, a_unit, b_unit, sbuf, rowbest,
           colbuf, colin, ktown, ktin, rowbuf, rowin, zrecv, zsend, yrecv, ysend, crecv, csend, arecv, asend, rrecv,
           rsend, krecv, ksend, mrecv, msend, lsem, osem):
    ns, nt, nz, chunks, cw, feats = dims
    s = lax.axis_index("src")
    t = lax.axis_index("tgt")
    z, y, c = s // 4, (s // 2) % 2, s % 2
    zy = s // 2
    right = (s + 4, t)
    left = (s - 4, t)
    over = (zy + 1 - 2 * y) * 2 + c
    rows = a_unit.shape[0]
    part = a_ref.shape[1]
    ow = colbuf.shape[2]
    has_right, has_left = z + 1 < nz, z >= 1

    def remote(src, dst, send, recv, where):
        return pltpu.make_async_remote_copy(
            src_ref=src, dst_ref=dst, send_sem=send, recv_sem=recv, device_id=where, device_id_type=MESH
        )

    local = pltpu.make_async_copy(x_ref, g.at[:, zy, c], lsem.at[0])
    local.start()
    acols = pl.ds(pl.multiple_of(t * part, part), part)
    local_a = pltpu.make_async_copy(a_ref, a_whole.at[:, acols], lsem.at[1])
    local_a.start()

    barrier = pltpu.get_barrier_semaphore()
    for k in range(1, ns):
        pl.semaphore_signal(barrier, inc=1, device_id=(lax.rem(s + k, ns), t), device_id_type=MESH)
    for k in range(1, nt):
        pl.semaphore_signal(barrier, inc=1, device_id=(s, lax.rem(t + k, nt)), device_id_type=MESH)
    pl.semaphore_wait(barrier, ns - 1 + nt - 1)

    def to_right(j, zp, own):
        ref = g.at[j, zp * 2 + y, c]
        return remote(x_ref.at[j] if own else ref, ref, zsend.at[0, j, zp], zrecv.at[j, zp], right)

    def to_left(j, zp, own):
        ref = g.at[j, zp * 2 + y, c]
        return remote(x_ref.at[j] if own else ref, ref, zsend.at[1, j, zp], zrecv.at[j, zp], left)

    def to_over(j, zp, own):
        ref = g.at[j, zp * 2 + y, c]
        return remote(x_ref.at[j] if own else ref, ref, ysend.at[j, zp], yrecv.at[j, zp], (over, t))

    def from_over(j, zp):
        ref = g.at[j, zp * 2 + 1 - y, c]
        return remote(ref, ref, ysend.at[j, zp], yrecv.at[j, zp], (over, t))

    def to_core(j):
        ref = g.at[j, :, c]
        return remote(ref, ref, csend.at[j], crecv.at[j], (s + 1 - 2 * c, t))

    def from_core(j):
        ref = g.at[j, :, 1 - c]
        return remote(ref, ref, csend.at[j], crecv.at[j], (s + 1 - 2 * c, t))

    def start_own(j):
        @pl.when(has_right)
        def _():
            to_right(j, z, True).start()

        @pl.when(has_left)
        def _():
            to_left(j, z, True).start()

    def to_tgt(k):
        return remote(a_ref, a_whole.at[:, acols], asend.at[k], arecv.at[t], (s, lax.rem(t + k, nt)))

    ahead = min(2, chunks)
    for j in range(ahead):
        start_own(j)
    for k in range(1, nt):
        to_tgt(k).start()
    local.wait()

    def normalize_sources():
        local_a.wait()
        for k in range(1, nt):
            other = lax.rem(t + k, nt)
            cols = pl.ds(pl.multiple_of(other * part, part), part)
            remote(a_ref, a_whole.at[:, cols], asend.at[k], arecv.at[other], (s, other)).wait_recv()
        block = 16

        def step(r, carry):
            at = pl.ds(pl.multiple_of(r * block, block), block)
            v = a_whole[at, :].astype(jnp.float32)
            scale = jnp.sqrt(jnp.sum(v * v, axis=1, keepdims=True) + epsilon)
            a_unit[at, :] = (v / scale).astype(jnp.bfloat16)
            return carry

        lax.fori_loop(0, rows // block, step, 0)
        for k in range(4):
            rowbest[k] = jnp.full(rowbest.shape[1:], -jnp.inf, jnp.float32)

    def out_copy(j):
        at = pl.ds(pl.multiple_of(j * cw, cw), cw)
        return pltpu.make_async_copy(sbuf.at[j % 2], s_out.at[:, at], osem.at[j % 2])

    def compute(j):
        def squares(k, acc):
            v = g[j, k // 2, k % 2].astype(jnp.float32)
            return acc + jnp.sum((v * v).reshape(feats // 8, 8, cw), axis=0)

        acc = lax.fori_loop(0, ns, squares, jnp.zeros((8, cw), jnp.float32))
        inverse = 1.0 / jnp.sqrt(jnp.sum(acc, axis=0, keepdims=True) + epsilon)

        def scale(k, carry):
            v = g[j, k // 2, k % 2].astype(jnp.float32)
            b_unit[pl.ds(pl.multiple_of(k * feats, feats), feats), :] = (v * inverse).astype(jnp.bfloat16)
            return carry

        lax.fori_loop(0, ns, scale, 0)

        @pl.when(j >= 2)
        def _():
            out_copy(j - 2).wait()

        slot = j % 2
        sbuf[slot] = jnp.dot(a_unit[...], b_unit[...], preferred_element_type=jnp.float32)
        tids = tid_ref[j]

        def group(r, best):
            at = pl.ds(pl.multiple_of(r * 8, 8), 8)
            ids = sid_ref[at, :]
            row = tuple(rowbest[k, at, :] for k in range(4))
            pieces = []
            for q in range(cw // 128):
                lanes = pl.ds(q * 128, 128)
                v = sbuf[slot, at, lanes]
                v = jnp.where(ids == tids[:, q * 128 : (q + 1) * 128], jnp.float32(excluded_score), v)
                row = insert(row, v)
                sbuf[slot, at, lanes] = v
                pieces.append(v)
            for k in range(4):
                rowbest[k, at, :] = row[k]
            return tuple(insert(best[q], pieces[q]) for q in range(cw // 128))

        best = lax.fori_loop(0, rows // 8, group, tuple(lowest((8, 128)) for _ in range(cw // 128)), unroll=2)
        out_copy(j).start()
        per = ow // 128
        for q in range(cw // 128):
            colbuf[j * (cw // ow) + q // per, :, (q % per) * 128 : (q % per + 1) * 128] = stacked(fold_sublanes(best[q]))

    def tick(i, carry):
        @pl.when(i + ahead < chunks)
        def _():
            start_own(i + ahead)

        @pl.when(i < chunks)
        def _():
            to_over(i, z, True).start()
            for d in range(1, nz):
                @pl.when(z - d >= 0)
                def _():
                    to_right(i, z - d, False).wait_recv()

                    @pl.when(has_right)
                    def _():
                        to_right(i, z - d, False).start()

                    to_over(i, z - d, False).start()

                @pl.when(z + d < nz)
                def _():
                    to_left(i, z + d, False).wait_recv()

                    @pl.when(has_left)
                    def _():
                        to_left(i, z + d, False).start()

                    to_over(i, z + d, False).start()

        @pl.when(jnp.logical_and(i >= 1, i <= chunks))
        def _():
            for zp in range(nz):
                from_over(i - 1, zp).wait_recv()
            to_core(i - 1).start()

        @pl.when(i == 2)
        def _():
            normalize_sources()

        @pl.when(i >= 2)
        def _():
            from_core(i - 2).wait_recv()
            compute(i - 2)

        return carry

    lax.fori_loop(0, chunks + 2, tick, 0)

    def col_copy(k):
        other = lax.rem(s + k, ns)
        return remote(colbuf.at[other], colin.at[s], ksend.at[k], krecv.at[s], (other, t))

    for k in range(1, ns):
        col_copy(k).start()
    colin[s] = colbuf[s]


    best = lowest((8, rows))
    for k in range(4):
        flat = rowbest[k].T
        for q in range(128 // 8):
            best = insert(best, flat[q * 8 : (q + 1) * 8, :])
    rowbuf[...] = stacked(fold_sublanes(best))
    rowin[t] = rowbuf[...]

    def row_copy(k):
        other = lax.rem(t + k, nt)
        return remote(rowbuf, rowin.at[t], rsend.at[k], rrecv.at[t], (s, other))

    for k in range(1, nt):
        row_copy(k).start()

    for k in range(1, ns):
        other = lax.rem(s + k, ns)
        remote(colbuf.at[0], colin.at[other], ksend.at[k], krecv.at[other], (other, t)).wait_recv()
    best = lowest((8, ow))
    for p in range(ns):
        best = insert(best, colin[p])
    best = fold_sublanes(best)
    ktown[...] = (best[0] + best[1] + best[2] + best[3]) * 0.25

    def mean_copy(k):
        other = lax.rem(s + k, ns)
        return remote(ktown, ktin.at[s], msend.at[k], mrecv.at[s], (other, t))

    for k in range(1, ns):
        mean_copy(k).start()
    ktin[s] = ktown[...]

    for k in range(1, nt):
        other = lax.rem(t + k, nt)
        remote(rowbuf, rowin.at[other], rsend.at[k], rrecv.at[other], (s, other)).wait_recv()
    best = lowest((8, rows))
    for p in range(nt):
        best = insert(best, rowin[p])
    best = fold_sublanes(best)
    ks_out[...] = (best[0] + best[1] + best[2] + best[3]) * 0.25

    def drain(j, carry):
        for zp in range(nz):
            @pl.when(jnp.logical_and(has_right, zp <= z))
            def _():
                to_right(j, zp, False).wait_send()

            @pl.when(jnp.logical_and(has_left, zp >= z))
            def _():
                to_left(j, zp, False).wait_send()

            to_over(j, zp, False).wait_send()
        to_core(j).wait_send()
        return carry

    lax.fori_loop(0, chunks, drain, 0)
    for j in range(max(0, chunks - 2), chunks):
        out_copy(j).wait()
    for k in range(1, nt):
        to_tgt(k).wait_send()
        row_copy(k).wait_send()
    for k in range(1, ns):
        col_copy(k).wait_send()
        mean_copy(k).wait_send()
    for k in range(1, ns):
        other = lax.rem(s + k, ns)
        remote(ktown, ktin.at[other], msend.at[k], mrecv.at[other], (other, t)).wait_recv()
    kt_out[...] = ktin[...]


def body(ns, nt, src_emb, tgt_emb, src_ids, tgt_ids):
    rows, part = src_emb.shape
    cols, feats = tgt_emb.shape
    width = part * nt
    nz = ns // 4
    cw = min(CHUNK, cols)
    chunks = cols // cw
    ow = cols // ns
    x = tgt_emb.reshape(chunks, cw, feats).transpose(0, 2, 1)
    sid = jnp.broadcast_to(src_ids[:, None], (rows, 128))
    tid = jnp.broadcast_to(tgt_ids.reshape(chunks, 1, cw), (chunks, 8, cw))
    f32, bf16 = jnp.float32, jnp.bfloat16
    dma = pltpu.SemaphoreType.DMA
    vmem = pl.BlockSpec(memory_space=pltpu.VMEM)
    scores, kt, ks = pl.pallas_call(
        functools.partial(kernel, (ns, nt, nz, chunks, cw, feats)),
        out_shape=(
            jax.ShapeDtypeStruct((rows, cols), f32),
            jax.ShapeDtypeStruct((ns, 8, ow), f32),
            jax.ShapeDtypeStruct((8, rows), f32),
        ),
        in_specs=[vmem] * 4,
        out_specs=(pl.BlockSpec(memory_space=pl.ANY), vmem, vmem),
        scratch_shapes=[
            pltpu.VMEM((chunks, ns // 2, 2, feats, cw), bf16),
            pltpu.VMEM((rows, width), bf16),
            pltpu.VMEM((rows, width), bf16),
            pltpu.VMEM((width, cw), bf16),
            pltpu.VMEM((2, rows, cw), f32),
            pltpu.VMEM((4, rows, 128), f32),
            pltpu.VMEM((ns, 8, ow), f32),
            pltpu.VMEM((ns, 8, ow), f32),
            pltpu.VMEM((8, ow), f32),
            pltpu.VMEM((ns, 8, ow), f32),
            pltpu.VMEM((8, rows), f32),
            pltpu.VMEM((nt, 8, rows), f32),
            dma((chunks, nz)),
            dma((2, chunks, nz)),
            dma((chunks, nz)),
            dma((chunks, nz)),
            dma((chunks,)),
            dma((chunks,)),
            dma((nt,)),
            dma((nt,)),
            dma((nt,)),
            dma((nt,)),
            dma((ns,)),
            dma((ns,)),
            dma((ns,)),
            dma((ns,)),
            dma((2,)),
            dma((2,)),
        ],
        compiler_params=pltpu.CompilerParams(
            collective_id=0, has_side_effects=True, vmem_limit_bytes=32 * 2**20
        ),
    )(x, src_emb, sid, tid)
    knn_src = ks[0]
    knn_tgt = kt[:, 0, :].reshape(cols)
    ratio = scores / (0.5 * (knn_src[:, None] + knn_tgt[None, :]))
    return jnp.where(src_ids[:, None] == tgt_ids[None, :], jnp.float32(0.0), ratio)


def solution(mesh):
    return jax.shard_map(
        functools.partial(body, mesh.shape["src"], mesh.shape["tgt"]),
        mesh=mesh,
        in_specs=(P("src", "tgt"), P("tgt", "src"), P("src"), P("tgt")),
        out_specs=P("src", "tgt"),
        check_vma=False,
    )
```

```python
import functools

import jax
import jax.numpy as jnp
from jax import lax
from jax.experimental import pallas as pl
from jax.experimental.pallas import tpu as pltpu
from jax.sharding import PartitionSpec as P

epsilon = 1e-06
excluded_score = -2.0
MESH = pl.DeviceIdType.MESH
CHUNK = 512
EVERY = 8
OVER_AHEAD = 4
LAG = 1


def insert(best, value):
    out = []
    for level in best[:-1]:
        out.append(jnp.maximum(level, value))
        value = jnp.minimum(level, value)
    out.append(jnp.maximum(best[-1], value))
    return tuple(out)


def merge(first, second):
    c = [jnp.maximum(first[k], second[3 - k]) for k in range(4)]
    a, b = jnp.maximum(c[0], c[2]), jnp.maximum(c[1], c[3])
    d, e = jnp.minimum(c[0], c[2]), jnp.minimum(c[1], c[3])
    return (jnp.maximum(a, b), jnp.minimum(a, b), jnp.maximum(d, e), jnp.minimum(d, e))


def fold_sublanes(best):
    for shift in (4, 2, 1):
        best = merge(best, tuple(pltpu.roll(level, shift, 0) for level in best))
    return best


def stacked(best):
    row = lax.broadcasted_iota(jnp.int32, best[0].shape, 0)
    low = jnp.full(best[0].shape, -jnp.inf, jnp.float32)
    for k in range(3, -1, -1):
        low = jnp.where(row == k, best[k], low)
    return low


def lowest(shape):
    return tuple(jnp.full(shape, -jnp.inf, jnp.float32) for _ in range(4))


def kernel(dims, x_ref, a_ref, sid_ref, tid_ref, s_out, kt_out, ks_out, sids, g, a_whole, a_unit, b_unit, sbuf, rowbest,
           colbuf, colin, ktown, ktin, rowbuf, rowin, zrecv, zsend, yrecv, ysend, crecv, csend, arecv, asend, rrecv,
           rsend, krecv, ksend, mrecv, msend, lsem, osem):
    ns, nt, nz, chunks, cw, feats = dims
    s = lax.axis_index("src")
    t = lax.axis_index("tgt")
    z, y, c = s // 4, (s // 2) % 2, s % 2
    right = (s + 4, t)
    left = (s - 4, t)
    over = (z * 4 + (1 - y) * 2 + c, t)
    core = (s + 1 - 2 * c, t)
    rows = a_unit.shape[0]
    part = a_ref.shape[1]
    ow = colbuf.shape[2]
    has_right, has_left = z + 1 < nz, z >= 1

    def remote(src, dst, send, recv, where):
        return pltpu.make_async_remote_copy(
            src_ref=src, dst_ref=dst, send_sem=send, recv_sem=recv, device_id=where, device_id_type=MESH
        )

    def chunk_cols(j):
        return pl.ds(pl.multiple_of(j * cw, cw), cw)

    local = [
        pltpu.make_async_copy(x_ref.at[:, j * cw : (j + 1) * cw], g.at[j, z, y, c], lsem.at[1 + j]) for j in range(chunks)
    ]
    for copy in local:
        copy.start()
    acols = pl.ds(pl.multiple_of(t * part, part), part)
    local_a = pltpu.make_async_copy(a_ref, a_whole.at[:, acols], lsem.at[0])
    local_a.start()

    barrier = pltpu.get_barrier_semaphore()

    @pl.when(has_right)
    def _():
        pl.semaphore_signal(barrier, inc=1, device_id=right, device_id_type=MESH)

    @pl.when(has_left)
    def _():
        pl.semaphore_signal(barrier, inc=1, device_id=left, device_id_type=MESH)

    pl.semaphore_signal(barrier, inc=1, device_id=over, device_id_type=MESH)
    pl.semaphore_signal(barrier, inc=1, device_id=core, device_id_type=MESH)
    for k in range(1, nt):
        pl.semaphore_signal(barrier, inc=1, device_id=(s, lax.rem(t + k, nt)), device_id_type=MESH)
    pl.semaphore_wait(barrier, 1 + nt + has_right.astype(jnp.int32) + has_left.astype(jnp.int32))

    def y_first(j):
        return lax.rem(j, EVERY) == EVERY - 1

    def to_right(j, zp, yy):
        ref = g.at[j, zp, yy, c]
        return remote(ref, ref, zsend.at[0, j, zp, yy], zrecv.at[j, zp, yy], right)

    def to_left(j, zp, yy):
        ref = g.at[j, zp, yy, c]
        return remote(ref, ref, zsend.at[1, j, zp, yy], zrecv.at[j, zp, yy], left)

    def to_over(j, zp):
        ref = g.at[j, zp, y, c]
        return remote(ref, ref, ysend.at[j, zp], yrecv.at[j, zp], over)

    def from_over(j, zp):
        ref = g.at[j, zp, 1 - y, c]
        return remote(ref, ref, ysend.at[j, zp], yrecv.at[j, zp], over)

    def to_core(j, yy):
        ref = g.at[j, :, yy, c]
        return remote(ref, ref, csend.at[j, yy], crecv.at[j, yy], core)

    def from_core(j, yy):
        ref = g.at[j, :, yy, 1 - c]
        return remote(ref, ref, csend.at[j, yy], crecv.at[j, yy], core)

    def start_z(j, yy):
        @pl.when(has_right)
        def _():
            to_right(j, z, yy).start()

        @pl.when(has_left)
        def _():
            to_left(j, z, yy).start()

    def to_tgt(k):
        return remote(a_ref, a_whole.at[:, acols], asend.at[k], arecv.at[t], (s, lax.rem(t + k, nt)))

    ahead = min(2, chunks)
    behind = nz - 1 + LAG
    for copy in local:
        copy.wait()
    for j in range(ahead):
        start_z(j, y)
    for j in range(chunks):
        if j < OVER_AHEAD or j % EVERY == EVERY - 1:
            to_over(j, z).start()
    for k in range(1, nt):
        to_tgt(k).start()
    sids[...] = jnp.broadcast_to(sid_ref[...], (128, rows)).T

    def normalize_sources():
        local_a.wait()
        for k in range(1, nt):
            other = lax.rem(t + k, nt)
            cols = pl.ds(pl.multiple_of(other * part, part), part)
            remote(a_ref, a_whole.at[:, cols], asend.at[k], arecv.at[other], (s, other)).wait_recv()
        block = 16

        def step(r, carry):
            at = pl.ds(pl.multiple_of(r * block, block), block)
            v = a_whole[at, :].astype(jnp.float32)
            scale = jnp.sqrt(jnp.sum(v * v, axis=1, keepdims=True) + epsilon)
            a_unit[at, :] = (v / scale).astype(jnp.bfloat16)
            return carry

        lax.fori_loop(0, rows // block, step, 0)
        for k in range(4):
            rowbest[k] = jnp.full(rowbest.shape[1:], -jnp.inf, jnp.float32)

    def out_copy(j):
        return pltpu.make_async_copy(sbuf.at[j % 2], s_out.at[:, chunk_cols(j)], osem.at[j % 2])

    def compute(j):
        def squares(k, acc):
            v = g[j, k // 4, (k // 2) % 2, k % 2].astype(jnp.float32)
            return acc + jnp.sum((v * v).reshape(feats // 8, 8, cw), axis=0)

        acc = lax.fori_loop(0, ns, squares, jnp.zeros((8, cw), jnp.float32))
        inverse = 1.0 / jnp.sqrt(jnp.sum(acc, axis=0, keepdims=True) + epsilon)

        def scale(k, carry):
            v = g[j, k // 4, (k // 2) % 2, k % 2].astype(jnp.float32)
            b_unit[pl.ds(pl.multiple_of(k * feats, feats), feats), :] = (v * inverse).astype(jnp.bfloat16)
            return carry

        lax.fori_loop(0, ns, scale, 0)

        @pl.when(j >= 2)
        def _():
            out_copy(j - 2).wait()

        slot = j % 2
        sbuf[slot] = jnp.dot(a_unit[...], b_unit[...], preferred_element_type=jnp.float32)
        tids = jnp.broadcast_to(tid_ref[:, chunk_cols(j)], (8, cw))

        def group(r, best):
            at = pl.ds(pl.multiple_of(r * 8, 8), 8)
            ids = sids[at, :]
            row = tuple(rowbest[k, at, :] for k in range(4))
            pieces = []
            for q in range(cw // 128):
                lanes = pl.ds(q * 128, 128)
                v = sbuf[slot, at, lanes]
                v = jnp.where(ids == tids[:, q * 128 : (q + 1) * 128], jnp.float32(excluded_score), v)
                row = insert(row, v)
                sbuf[slot, at, lanes] = v
                pieces.append(v)
            for k in range(4):
                rowbest[k, at, :] = row[k]
            return tuple(insert(best[q], pieces[q]) for q in range(cw // 128))

        best = lax.fori_loop(0, rows // 8, group, tuple(lowest((8, 128)) for _ in range(cw // 128)), unroll=2)
        out_copy(j).start()
        per = ow // 128
        for q in range(cw // 128):
            colbuf[j * (cw // ow) + q // per, :, (q % per) * 128 : (q % per + 1) * 128] = stacked(fold_sublanes(best[q]))

    def within(j):
        return jnp.logical_and(j >= 0, j < chunks)

    def stage(j, d, first):
        both = (y, 1 - y) if first else (y,)

        @pl.when(z - d >= 0)
        def _():
            for yy in both:
                to_right(j, z - d, yy).wait_recv()

                @pl.when(has_right)
                def _():
                    to_right(j, z - d, yy).start()

            if not first:
                to_over(j, z - d).start()

        @pl.when(z + d < nz)
        def _():
            for yy in both:
                to_left(j, z + d, yy).wait_recv()

                @pl.when(has_left)
                def _():
                    to_left(j, z + d, yy).start()

            if not first:
                to_over(j, z + d).start()

        if d == nz - 1:
            for yy in both:
                to_core(j, yy).start()

    def tick(i, carry):
        @pl.when(i + ahead < chunks)
        def _():
            start_z(i + ahead, y)

            @pl.when(y_first(i + ahead))
            def _():
                from_over(i + ahead, z).wait_recv()
                start_z(i + ahead, 1 - y)

        @pl.when(jnp.logical_and(i + OVER_AHEAD < chunks, jnp.logical_not(y_first(i + OVER_AHEAD))))
        def _():
            to_over(i + OVER_AHEAD, z).start()

        for d in range(1, nz):
            j = i - d + 1

            @pl.when(jnp.logical_and(within(j), jnp.logical_not(y_first(j))))
            def _():
                stage(j, d, False)

            @pl.when(jnp.logical_and(within(j), y_first(j)))
            def _():
                stage(j, d, True)

        jy = i - nz + 1

        @pl.when(jnp.logical_and(within(jy), jnp.logical_not(y_first(jy))))
        def _():
            for zp in range(nz):
                from_over(jy, zp).wait_recv()
            to_core(jy, 1 - y).start()

        @pl.when(i == behind)
        def _():
            normalize_sources()

        @pl.when(i >= behind)
        def _():
            for yy in range(2):
                from_core(i - behind, yy).wait_recv()
            compute(i - behind)

        return carry

    lax.fori_loop(0, chunks + behind, tick, 0)

    def col_copy(k):
        other = lax.rem(s + k, ns)
        return remote(colbuf.at[other], colin.at[s], ksend.at[k], krecv.at[s], (other, t))

    for k in range(1, ns):
        col_copy(k).start()
    colin[s] = colbuf[s]


    best = lowest((8, rows))
    for k in range(4):
        flat = rowbest[k].T
        for q in range(128 // 8):
            best = insert(best, flat[q * 8 : (q + 1) * 8, :])
    rowbuf[...] = stacked(fold_sublanes(best))
    rowin[t] = rowbuf[...]

    def row_copy(k):
        other = lax.rem(t + k, nt)
        return remote(rowbuf, rowin.at[t], rsend.at[k], rrecv.at[t], (s, other))

    for k in range(1, nt):
        row_copy(k).start()

    for k in range(1, ns):
        other = lax.rem(s + k, ns)
        remote(colbuf.at[0], colin.at[other], ksend.at[k], krecv.at[other], (other, t)).wait_recv()
    best = lowest((8, ow))
    for p in range(ns):
        best = insert(best, colin[p])
    best = fold_sublanes(best)
    ktown[...] = (best[0] + best[1] + best[2] + best[3]) * 0.25

    def mean_copy(k):
        other = lax.rem(s + k, ns)
        return remote(ktown, ktin.at[s], msend.at[k], mrecv.at[s], (other, t))

    for k in range(1, ns):
        mean_copy(k).start()
    ktin[s] = ktown[...]

    for k in range(1, nt):
        other = lax.rem(t + k, nt)
        remote(rowbuf, rowin.at[other], rsend.at[k], rrecv.at[other], (s, other)).wait_recv()
    best = lowest((8, rows))
    for p in range(nt):
        best = insert(best, rowin[p])
    best = fold_sublanes(best)
    ks_out[...] = (best[0] + best[1] + best[2] + best[3]) * 0.25

    def drain(j, carry):
        def drain_z(zp, yy):
            @pl.when(jnp.logical_and(has_right, zp <= z))
            def _():
                to_right(j, zp, yy).wait_send()

            @pl.when(jnp.logical_and(has_left, zp >= z))
            def _():
                to_left(j, zp, yy).wait_send()

        for zp in range(nz):
            drain_z(zp, y)

        @pl.when(y_first(j))
        def _():
            for zp in range(nz):
                drain_z(zp, 1 - y)
            to_over(j, z).wait_send()

        @pl.when(jnp.logical_not(y_first(j)))
        def _():
            for zp in range(nz):
                to_over(j, zp).wait_send()

        for yy in range(2):
            to_core(j, yy).wait_send()
        return carry

    lax.fori_loop(0, chunks, drain, 0)
    for j in range(max(0, chunks - 2), chunks):
        out_copy(j).wait()
    for k in range(1, nt):
        to_tgt(k).wait_send()
        row_copy(k).wait_send()
    for k in range(1, ns):
        col_copy(k).wait_send()
        mean_copy(k).wait_send()
    for k in range(1, ns):
        other = lax.rem(s + k, ns)
        remote(ktown, ktin.at[other], msend.at[k], mrecv.at[other], (other, t)).wait_recv()
    kt_out[...] = ktin[...]


def body(ns, nt, src_emb, tgt_emb, src_ids, tgt_ids):
    rows, part = src_emb.shape
    cols, feats = tgt_emb.shape
    width = part * nt
    nz = ns // 4
    cw = min(CHUNK, cols)
    chunks = cols // cw
    ow = cols // ns
    f32, bf16 = jnp.float32, jnp.bfloat16
    dma = pltpu.SemaphoreType.DMA
    hbm = pl.BlockSpec(memory_space=pl.ANY)
    vmem = pl.BlockSpec(memory_space=pltpu.VMEM)
    scores, kt, ks = pl.pallas_call(
        functools.partial(kernel, (ns, nt, nz, chunks, cw, feats)),
        out_shape=(
            jax.ShapeDtypeStruct((rows, cols), f32),
            jax.ShapeDtypeStruct((ns, 8, ow), f32),
            jax.ShapeDtypeStruct((8, rows), f32),
        ),
        in_specs=[hbm, hbm, vmem, vmem],
        out_specs=(hbm, vmem, vmem),
        scratch_shapes=[
            pltpu.VMEM((rows, 128), jnp.int32),
            pltpu.VMEM((chunks, nz, 2, 2, feats, cw), bf16),
            pltpu.VMEM((rows, width), bf16),
            pltpu.VMEM((rows, width), bf16),
            pltpu.VMEM((width, cw), bf16),
            pltpu.VMEM((2, rows, cw), f32),
            pltpu.VMEM((4, rows, 128), f32),
            pltpu.VMEM((ns, 8, ow), f32),
            pltpu.VMEM((ns, 8, ow), f32),
            pltpu.VMEM((8, ow), f32),
            pltpu.VMEM((ns, 8, ow), f32),
            pltpu.VMEM((8, rows), f32),
            pltpu.VMEM((nt, 8, rows), f32),
            dma((chunks, nz, 2)),
            dma((2, chunks, nz, 2)),
            dma((chunks, nz)),
            dma((chunks, nz)),
            dma((chunks, 2)),
            dma((chunks, 2)),
            dma((nt,)),
            dma((nt,)),
            dma((nt,)),
            dma((nt,)),
            dma((ns,)),
            dma((ns,)),
            dma((ns,)),
            dma((ns,)),
            dma((1 + chunks,)),
            dma((2,)),
        ],
        compiler_params=pltpu.CompilerParams(
            collective_id=0, has_side_effects=True, vmem_limit_bytes=32 * 2**20
        ),
    )(tgt_emb.T, src_emb, src_ids.reshape(1, rows), tgt_ids.reshape(1, cols))
    knn_src = ks[0]
    knn_tgt = kt[:, 0, :].reshape(cols)
    ratio = scores / (0.5 * (knn_src[:, None] + knn_tgt[None, :]))
    return jnp.where(src_ids[:, None] == tgt_ids[None, :], jnp.float32(0.0), ratio)


def solution(mesh):
    return jax.shard_map(
        functools.partial(body, mesh.shape["src"], mesh.shape["tgt"]),
        mesh=mesh,
        in_specs=(P("src", "tgt"), P("tgt", "src"), P("src"), P("tgt")),
        out_specs=P("src", "tgt"),
        check_vma=False,
    )
```
